128 devices in a mesh: outer: 2 (over core), inner: 64 (over y, x, z).
Axes of the slice: x: 4, y: 4, z: 4, core: 2. Of those that a mesh axis runs over, the one named last changes fastest.
Arguments:
- features: float32 [262144, 1024], P(('outer', 'inner'))
- dest: int32 [8192], P(('outer', 'inner')), may hold values from 0 to 63, as said below
- slot: int32 [8192], P(('outer', 'inner')), may hold values from 0 to 63, as said below
Outputs:
- standardized: float32 [262144, 1024], P(('outer', 'inner'))
- moments: float32 [2, 1024], replicated
The draws below stay inside these ranges and needn't reach their ends.
Inputs may be any that keep to these rules, and one draw needn't show every extreme that they name: `dest`: blocks of one device name destinations in the same shuffle domain; from one device at most 1 block go to any one destination, and exactly 1 to each destination it names. Every device of a shuffle domain receives exactly 64 blocks, each with a different slot.
All inputs are finite; a program needn't handle non-finite values.
Results may differ from the reference program's by a relative error of at most 0.000031.
Values sent between devices are 32-bit elements; how exact they have to be, the bound alone decides.
A program may use at most 128 MiB of HBM per device.

```python
import jax
import jax.numpy as jnp
from jax import lax

F = 1024
ROWS_DEV = 2048
BLOCK = 32
BLK_DEV = 64
PEERS = 64
ROWS = 262144
BLOCKS = 8192
DEVICES = 128


def route_table(key):
    group_total = BLOCKS // (PEERS * BLK_DEV)

    def one_group(group):
        group_key = jax.random.fold_in(jax.random.fold_in(key, 7), group)
        offsets = jax.random.permutation(jax.random.fold_in(group_key, 1), PEERS)
        ordering = jax.random.permutation(jax.random.fold_in(group_key, 2), BLK_DEV)
        turning = jax.random.permutation(jax.random.fold_in(group_key, 3), BLK_DEV)
        relabel = jax.random.permutation(jax.random.fold_in(group_key, 4), PEERS)
        inverse = jnp.argsort(relabel)
        offset_of = offsets[ordering % PEERS]
        sources = jnp.arange(PEERS)
        targets = relabel[(inverse[sources][:, None] + offset_of[None, :]) % PEERS]
        slot_table = (turning[None, :] + targets) % BLK_DEV
        return (targets.reshape(-1), slot_table.reshape(-1))
    targets, slot_table = jax.vmap(one_group)(jnp.arange(group_total))
    return (targets.reshape(-1).astype(jnp.int32), slot_table.reshape(-1).astype(jnp.int32))


def draw_dest(key, part):
    return route_table(key)[0]


def draw_slot(key, part):
    return route_table(key)[1]


def draw_features(key, part):
    column_scale = 10.0 ** jax.random.uniform(jax.random.fold_in(key, 1), (1, F))
    column_shift = 3.0 * jax.random.normal(jax.random.fold_in(key, 2), (1, F))
    row_scale = 10.0 ** jax.random.uniform(jax.random.fold_in(key, 3), (ROWS, 1))
    progress = jnp.arange(ROWS, dtype=jnp.float32)[:, None] / (ROWS - 1)
    jitter = jnp.clip(jax.random.normal(jax.random.fold_in(key, 5), (ROWS, F)), -6.0, 6.0)
    values = column_shift + column_scale * (6.0 + 12.0 * progress + row_scale * jitter)
    return values.astype(jnp.float32)


def setup_inputs(seed: int = 0) -> dict:
    arg_keys = jax.random.split(jax.random.key(seed), 4)
    return {
        "features": draw_features(jax.random.fold_in(arg_keys[3], 71), 0),
        "dest": draw_dest(jax.random.fold_in(arg_keys[3], 71), 0),
        "slot": draw_slot(jax.random.fold_in(arg_keys[3], 71), 0),
    }


eps_value = 1e-06
clip_value = 3.0

def merge_pair(center_a, spread_a, center_b, spread_b, half):
    gap = center_b - center_a
    return ((center_a + center_b) * 0.5, spread_a + spread_b + gap * gap * half)

def merge_levels(centers, spreads, row_count):
    level_count = row_count
    while centers.shape[0] > 1:
        paired_c = centers.reshape(-1, 2, centers.shape[1])
        paired_s = spreads.reshape(-1, 2, spreads.shape[1])
        centers, spreads = merge_pair(paired_c[:, 0], paired_s[:, 0], paired_c[:, 1], paired_s[:, 1], level_count * 0.5)
        level_count = level_count * 2
    return (centers[0], spreads[0])

def local_moments(block_rows):
    center = lax.optimization_barrier(jnp.mean(block_rows, axis=0))
    deviation = block_rows - center
    return (center, lax.optimization_barrier(jnp.sum(deviation * deviation, axis=0)))

def standardize(block_rows, center, factor):
    return jnp.clip((block_rows - center) * factor, -clip_value, clip_value)

def reference(features, dest, slot):
    total_rows = features.shape[0]
    shards = features.reshape(DEVICES, ROWS_DEV, F)
    centers, spreads = lax.map(local_moments, shards)
    center, spread = merge_levels(centers, spreads, ROWS_DEV)
    variance = spread / total_rows
    factor = lax.rsqrt(variance + eps_value)
    scaled = lax.map(lambda block_rows: standardize(block_rows, center, factor), shards)
    group_size = PEERS * BLK_DEV
    block_ids = jnp.arange(BLOCKS, dtype=jnp.int32)
    target = block_ids // group_size * group_size + dest.astype(jnp.int32) * BLK_DEV + slot.astype(jnp.int32)
    placed = jnp.zeros((BLOCKS, BLOCK, F), jnp.float32).at[target].set(scaled.reshape(BLOCKS, BLOCK, F))
    return (placed.reshape(total_rows, F), jnp.stack([center, variance]))
```

```python
import functools
import itertools

import jax
import jax.numpy as jnp
from jax import lax
from jax.experimental import pallas as pl
from jax.experimental.pallas import tpu as pltpu
from jax.sharding import PartitionSpec as P

MESH = pl.DeviceIdType.MESH
eps_value = 1e-06
clip_value = 3.0
SIDE = 4
PIECES = 8
WINDOW = 21
LOADS = 8
LANES = 128


def hops(offset):
    return sum(min(v, SIDE - v) for v in offset)


def send_order():
    left = [d for d in itertools.product(range(SIDE), repeat=3) if any(d)]
    groups = []
    while left:
        first, group = left[0], []
        for shift in range(3):
            for sign in (1, -1):
                d = tuple(sign * first[(j + shift) % 3] % SIDE for j in range(3))
                if d in left:
                    left.remove(d)
                    group.append(d)
        groups.append(group)
    return [d for group in sorted(groups, key=lambda g: hops(g[0])) for d in group]


def merge_pair(a, b, half):
    gap = b[0] - a[0]
    return ((a[0] + b[0]) * 0.5, a[1] + b[1] + gap * gap * half)


def exchange_kernel(
    dest_ref, slot_ref, feat_hbm,
    land_ref, slots_ref, stat_ref,
    feats, stage, order_v, slot_v, order_s, moment, peer_moment,
    load_sem, order_sem, send_sem, land_sem, slot_send, slot_recv, mom_send, mom_recv,
):
    peers, rows, width = land_ref.shape
    tiles = width // LANES
    piece = rows // PIECES if rows // PIECES >= 8 else 8
    row_pieces = rows // piece
    col_pieces = PIECES // row_pieces
    cols = width // col_pieces
    core, me = lax.axis_index("outer"), lax.axis_index("inner")
    y, x, z = me // (SIDE * SIDE), (me // SIDE) % SIDE, me % SIDE

    def at(offset):
        dy, dx, dz = offset
        return ((y + dy) % SIDE) * SIDE * SIDE + ((x + dx) % SIDE) * SIDE + (z + dz) % SIDE

    barrier = pltpu.get_barrier_semaphore()

    def greet(k, carry):
        pl.semaphore_signal(barrier, inc=1, device_id=(core, me ^ k), device_id_type=MESH)
        return carry

    lax.fori_loop(1, peers, greet, 0)
    pl.semaphore_signal(barrier, inc=1, device_id=(1 - core, me), device_id_type=MESH)

    load = peers // LOADS
    loads = [
        pltpu.make_async_copy(
            feat_hbm.at[pl.ds(k * load, load)], feats.at[pl.ds(k * load, load)], load_sem.at[k]
        )
        for k in range(LOADS)
    ]
    for copy in loads:
        copy.start()

    blocks = dest_ref.shape[1]
    hit = dest_ref[...] == lax.broadcasted_iota(jnp.int32, (peers, blocks), 0)
    ids = lax.broadcasted_iota(jnp.int32, (peers, blocks), 1)
    order = jnp.max(jnp.where(hit, ids, 0), axis=1, keepdims=True)
    slots = jnp.max(jnp.where(hit, slot_ref[...], 0), axis=1, keepdims=True)
    order_v[...] = jnp.broadcast_to(order, order_v.shape)
    slot_v[...] = jnp.broadcast_to(slots, slot_v.shape)
    to_scalar = pltpu.make_async_copy(order_v, order_s, order_sem)
    to_scalar.start()
    to_scalar.wait()
    for copy in loads:
        copy.wait()

    def arrange(p, carry):
        stage[p] = feats[order_s[p, 0]]
        return carry

    lax.fori_loop(0, peers, arrange, 0)
    land_ref[me] = feats[order_s[me, 0]]
    slots_ref[pl.ds(me, 1)] = slot_v[pl.ds(me, 1)]

    pl.semaphore_wait(barrier, peers)

    def local_moments():
        def total(b, acc):
            block = feats[b]
            for r in range(0, rows, 8):
                acc = acc + block[r : r + 8]
            return acc

        zero = jnp.zeros((8, width), jnp.float32)
        count = peers * rows
        center = jnp.sum(lax.fori_loop(0, peers, total, zero), axis=0, keepdims=True) * (1.0 / count)
        wide = jnp.broadcast_to(center, (8, width))

        def squares(b, acc):
            block = feats[b]
            for r in range(0, rows, 8):
                gap = block[r : r + 8] - wide
                acc = acc + gap * gap
            return acc

        spread = jnp.sum(lax.fori_loop(0, peers, squares, zero), axis=0, keepdims=True)
        for t in range(tiles):
            moment[0, pl.ds(t, 1)] = center[:, t * LANES : (t + 1) * LANES]
            moment[0, pl.ds(tiles + t, 1)] = spread[:, t * LANES : (t + 1) * LANES]

    def read(ref):
        return ref[pl.ds(0, tiles)], ref[pl.ds(tiles, tiles)]

    def write(ref, pair):
        ref[pl.ds(0, tiles)] = pair[0]
        ref[pl.ds(tiles, tiles)] = pair[1]

    def moment_copies(step):
        if step == 3:
            targets = [(1 - core, me)]
        else:
            targets = [(core, me ^ (k * SIDE**step)) for k in (1, 2, 3)]
        return [
            pltpu.make_async_remote_copy(
                src_ref=moment.at[step],
                dst_ref=peer_moment.at[step * 3 + k],
                send_sem=mom_send.at[step * 3 + k],
                recv_sem=mom_recv.at[step * 3 + k],
                device_id=target,
                device_id_type=MESH,
            )
            for k, target in enumerate(targets)
        ]

    def moment_send(step):
        for copy in moment_copies(step):
            copy.start()

    def moment_merge(step):
        for copy in moment_copies(step):
            copy.wait()
        count = float(peers * rows * SIDE**step)
        pair = merge_pair(read(moment.at[step]), read(peer_moment.at[step * 3]), count * 0.5)
        if step < 3:
            other = merge_pair(
                read(peer_moment.at[step * 3 + 1]), read(peer_moment.at[step * 3 + 2]), count * 0.5
            )
            pair = merge_pair(pair, other, count)
            write(moment.at[step + 1], pair)
            moment_send(step + 1)
        else:
            write(stat_ref, (pair[0], pair[1] / (count * 2.0)))

    targets = [at(d) for d in send_order()]

    def slot_copy(j):
        return pltpu.make_async_remote_copy(
            src_ref=slot_v.at[pl.ds(targets[j], 1)],
            dst_ref=slots_ref.at[pl.ds(me, 1)],
            send_sem=slot_send.at[j],
            recv_sem=slot_recv,
            device_id=(core, targets[j]),
            device_id_type=MESH,
        )

    def piece_copy(q, j):
        part = (pl.ds((q // col_pieces) * piece, piece), pl.ds(pl.multiple_of((q % col_pieces) * cols, cols), cols))
        return pltpu.make_async_remote_copy(
            src_ref=stage.at[(targets[j],) + part],
            dst_ref=land_ref.at[(me,) + part],
            send_sem=send_sem.at[j % WINDOW],
            recv_sem=land_sem,
            device_id=(core, targets[j]),
            device_id_type=MESH,
        )

    def run(q, carry):
        for j in range(peers - 1):
            if j < WINDOW:

                @pl.when(q > 0)
                def _():
                    piece_copy(q, j).wait_send()
            else:
                piece_copy(q, j).wait_send()
            piece_copy(q, j).start()
            if j == WINDOW - 1:

                @pl.when(q == 0)
                def _():
                    local_moments()
                    moment_send(0)
                    for i in range(peers - 1):
                        slot_copy(i).start()

        for step in range(4):

            @pl.when(q == step + 1)
            def _():
                moment_merge(step)

        return carry

    lax.fori_loop(0, PIECES, run, 0)
    for j in range(WINDOW):
        piece_copy(0, j).wait_send()
    for j in range(peers - 1):
        slot_copy(j).wait_send()
    others = pl.ds(0, peers - 1)
    pltpu.make_async_copy(slots_ref.at[others], slots_ref.at[others], slot_recv).wait()
    pltpu.make_async_copy(land_ref.at[others], land_ref.at[others], land_sem).wait()


def finish_kernel(land_ref, slots_ref, stat_ref, out_hbm, mom_ref, ready, out_sem):
    peers, rows, width = land_ref.shape
    tiles = width // LANES
    row = lambda ref, first: jnp.concatenate([ref[pl.ds(first + t, 1)] for t in range(tiles)], axis=1)
    center, variance = row(stat_ref, 0), row(stat_ref, tiles)
    mom_ref[pl.ds(0, 1)] = center
    mom_ref[pl.ds(1, 1)] = variance
    factor = lax.rsqrt(variance + eps_value)
    center = jnp.broadcast_to(center, (8, width))
    factor = jnp.broadcast_to(factor, (8, width))

    def block(s, carry):
        for r in range(0, rows, 8):
            scaled = (land_ref[s, pl.ds(r, 8)] - center) * factor
            ready[s, pl.ds(r, 8)] = jnp.clip(scaled, -clip_value, clip_value)
        pltpu.make_async_copy(ready.at[s], out_hbm.at[slots_ref[s, 0]], out_sem).start()
        return carry

    lax.fori_loop(0, peers, block, 0)
    pltpu.make_async_copy(ready, out_hbm, out_sem).wait()


def body(features, dest, slot):
    row_count, width = features.shape
    peers = lax.axis_size("inner")
    blocks = dest.shape[0]
    rows = row_count // blocks
    tiles = width // LANES
    vmem = pl.BlockSpec(memory_space=pltpu.VMEM)
    hbm = pl.BlockSpec(memory_space=pltpu.HBM)
    smem = pl.BlockSpec(memory_space=pltpu.SMEM)
    landed, slots, stats = pl.pallas_call(
        exchange_kernel,
        out_shape=[
            pltpu.VMEM((peers, rows, width), jnp.float32),
            pltpu.VMEM((peers, LANES), jnp.int32),
            pltpu.VMEM((2 * tiles, LANES), jnp.float32),
        ],
        in_specs=[vmem, vmem, hbm],
        out_specs=[vmem, vmem, vmem],
        scratch_shapes=[
            pltpu.VMEM((blocks, rows, width), jnp.float32),
            pltpu.VMEM((peers, rows, width), jnp.float32),
            pltpu.VMEM((peers, LANES), jnp.int32),
            pltpu.VMEM((peers, LANES), jnp.int32),
            pltpu.SMEM((peers, LANES), jnp.int32),
            pltpu.VMEM((4, 2 * tiles, LANES), jnp.float32),
            pltpu.VMEM((10, 2 * tiles, LANES), jnp.float32),
            pltpu.SemaphoreType.DMA((LOADS,)),
            pltpu.SemaphoreType.DMA,
            pltpu.SemaphoreType.DMA((WINDOW,)),
            pltpu.SemaphoreType.DMA,
            pltpu.SemaphoreType.DMA((peers - 1,)),
            pltpu.SemaphoreType.DMA,
            pltpu.SemaphoreType.DMA((10,)),
            pltpu.SemaphoreType.DMA((10,)),
        ],
        compiler_params=pltpu.CompilerParams(
            collective_id=0, has_side_effects=True, vmem_limit_bytes=32 * 2**20
        ),
    )(dest.reshape(1, blocks), slot.reshape(1, blocks), features.reshape(blocks, rows, width))
    standardized, moments = pl.pallas_call(
        finish_kernel,
        out_shape=[
            jax.ShapeDtypeStruct((peers, rows, width), jnp.float32),
            jax.ShapeDtypeStruct((2, width), jnp.float32),
        ],
        in_specs=[vmem, smem, vmem],
        out_specs=[hbm, vmem],
        scratch_shapes=[
            pltpu.VMEM((peers, rows, width), jnp.float32),
            pltpu.SemaphoreType.DMA,
        ],
        compiler_params=pltpu.CompilerParams(vmem_limit_bytes=24 * 2**20),
    )(landed, slots, stats)
    return (standardized.reshape(row_count, width), moments)


def solution(mesh):
    in_specs = (P(("outer", "inner"), None), P(("outer", "inner")), P(("outer", "inner")))
    out_specs = (P(("outer", "inner"), None), P())
    return jax.shard_map(body, mesh=mesh, in_specs=in_specs, out_specs=out_specs, check_vma=False)
```

```python
import itertools

import jax
import jax.numpy as jnp
from jax import lax
from jax.experimental import pallas as pl
from jax.experimental.pallas import tpu as pltpu
from jax.sharding import PartitionSpec as P

MESH = pl.DeviceIdType.MESH
eps_value = 1e-06
clip_value = 3.0
SIDE = 4
PIECES = 8
LOADS = 8
LANES = 128


def hops(offset):
    return sum(min(v, SIDE - v) for v in offset)


def send_order():
    left = [d for d in itertools.product(range(SIDE), repeat=3) if any(d)]
    groups = []
    while left:
        first, group = left[0], []
        for shift in range(3):
            for sign in (1, -1):
                d = tuple(sign * first[(j + shift) % 3] % SIDE for j in range(3))
                if d in left:
                    left.remove(d)
                    group.append(d)
        groups.append(group)
    return [d for group in sorted(groups, key=lambda g: hops(g[0])) for d in group]


def merge_pair(a, b, half):
    gap = b[0] - a[0]
    return ((a[0] + b[0]) * 0.5, a[1] + b[1] + gap * gap * half)


def exchange_kernel(
    dest_hbm, slot_hbm, feat_hbm,
    land_ref, slots_ref, stat_ref,
    feats, stage, dest_v, slot_v, order_v, slots_v, order_s, moment, peer_moment,
    load_sem, send_sem, land_sem, slot_send, slot_recv, mom_send, mom_recv,
):
    peers, rows, width = land_ref.shape
    tiles = width // LANES
    col_pieces = PIECES * 8 // rows
    cols = width // col_pieces
    core, me = lax.axis_index("outer"), lax.axis_index("inner")
    y, x, z = me // (SIDE * SIDE), (me // SIDE) % SIDE, me % SIDE

    def at(offset):
        dy, dx, dz = offset
        return ((y + dy) % SIDE) * SIDE * SIDE + ((x + dx) % SIDE) * SIDE + (z + dz) % SIDE

    barrier = pltpu.get_barrier_semaphore()
    load = peers // LOADS
    loads = [
        pltpu.make_async_copy(
            feat_hbm.at[pl.ds(k * load, load)], feats.at[pl.ds(k * load, load)], load_sem.at[k]
        )
        for k in range(LOADS)
    ]
    small = [
        pltpu.make_async_copy(dest_hbm, dest_v, load_sem.at[LOADS]),
        pltpu.make_async_copy(slot_hbm, slot_v, load_sem.at[LOADS + 1]),
    ]
    for copy in small + loads:
        copy.start()

    def greet(k, carry):
        pl.semaphore_signal(barrier, inc=1, device_id=(core, me ^ k), device_id_type=MESH)
        return carry

    lax.fori_loop(1, peers, greet, 0)
    pl.semaphore_signal(barrier, inc=1, device_id=(1 - core, me), device_id_type=MESH)

    for copy in small:
        copy.wait()
    blocks = dest_v.shape[1]
    hit = dest_v[...] == lax.broadcasted_iota(jnp.int32, (peers, blocks), 0)
    ids = lax.broadcasted_iota(jnp.int32, (peers, blocks), 1)
    order = jnp.max(jnp.where(hit, ids, 0), axis=1, keepdims=True)
    slots = jnp.max(jnp.where(hit, slot_v[...], 0), axis=1, keepdims=True)
    order_v[...] = jnp.broadcast_to(order, order_v.shape)
    slots_v[...] = jnp.broadcast_to(slots, slots_v.shape)
    to_scalar = pltpu.make_async_copy(order_v, order_s, load_sem.at[LOADS + 2])
    to_scalar.start()
    slots_ref[pl.ds(me, 1)] = slots_v[pl.ds(me, 1)]

    zero = jnp.zeros((8, width), jnp.float32)
    acc = zero
    for k in range(LOADS):
        loads[k].wait()

        def total(b, acc):
            block = feats[b]
            for r in range(0, rows, 8):
                acc = acc + block[r : r + 8]
            return acc

        acc = lax.fori_loop(k * load, (k + 1) * load, total, acc)
    center = jnp.sum(acc, axis=0, keepdims=True) * (1.0 / (peers * rows))
    to_scalar.wait()

    def part(q):
        return pl.ds((q // col_pieces) * 8, 8), pl.ds(pl.multiple_of((q % col_pieces) * cols, cols), cols)

    def arrange(q):
        def one(p, carry):
            stage[(p,) + part(q)] = feats[(order_s[p, 0],) + part(q)]
            return carry

        lax.fori_loop(0, peers, one, 0, unroll=8)

    targets = [at(d) for d in send_order()]

    def slot_copy(j):
        return pltpu.make_async_remote_copy(
            src_ref=slots_v.at[pl.ds(targets[j], 1)],
            dst_ref=slots_ref.at[pl.ds(me, 1)],
            send_sem=slot_send.at[j],
            recv_sem=slot_recv,
            device_id=(core, targets[j]),
            device_id_type=MESH,
        )

    def piece_copy(q, j):
        return pltpu.make_async_remote_copy(
            src_ref=stage.at[(targets[j],) + part(q)],
            dst_ref=land_ref.at[(me,) + part(q)],
            send_sem=send_sem.at[j],
            recv_sem=land_sem,
            device_id=(core, targets[j]),
            device_id_type=MESH,
        )

    def read(ref):
        return ref[pl.ds(0, tiles)], ref[pl.ds(tiles, tiles)]

    def write(ref, pair):
        ref[pl.ds(0, tiles)] = pair[0]
        ref[pl.ds(tiles, tiles)] = pair[1]

    def moment_copies(step):
        if step == 3:
            mates = [(1 - core, me)]
        else:
            mates = [(core, me ^ (k * SIDE**step)) for k in (1, 2, 3)]
        return [
            pltpu.make_async_remote_copy(
                src_ref=moment.at[step],
                dst_ref=peer_moment.at[step * 3 + k],
                send_sem=mom_send.at[step * 3 + k],
                recv_sem=mom_recv.at[step * 3 + k],
                device_id=mate,
                device_id_type=MESH,
            )
            for k, mate in enumerate(mates)
        ]

    def moment_send(step):
        for copy in moment_copies(step):
            copy.start()

    def moment_merge(step):
        for copy in moment_copies(step):
            copy.wait()
        count = float(peers * rows * SIDE**step)
        pair = merge_pair(read(moment.at[step]), read(peer_moment.at[step * 3]), count * 0.5)
        if step < 3:
            other = merge_pair(
                read(peer_moment.at[step * 3 + 1]), read(peer_moment.at[step * 3 + 2]), count * 0.5
            )
            pair = merge_pair(pair, other, count)
            write(moment.at[step + 1], pair)
            moment_send(step + 1)
        else:
            write(stat_ref, (pair[0], pair[1] / (count * 2.0)))

    arrange(0)
    pl.semaphore_wait(barrier, peers)
    for j in range(peers - 1):
        piece_copy(0, j).start()
    arrange(1)
    wide = jnp.broadcast_to(center, (8, width))

    def squares(b, acc):
        block = feats[b]
        for r in range(0, rows, 8):
            gap = block[r : r + 8] - wide
            acc = acc + gap * gap
        return acc

    spread = jnp.sum(lax.fori_loop(0, peers, squares, zero), axis=0, keepdims=True)
    for t in range(tiles):
        moment[0, pl.ds(t, 1)] = center[:, t * LANES : (t + 1) * LANES]
        moment[0, pl.ds(tiles + t, 1)] = spread[:, t * LANES : (t + 1) * LANES]
    moment_send(0)
    land_ref[me] = feats[order_s[me, 0]]

    def run(q, carry):
        for j in range(peers - 1):
            piece_copy(q - 1, j).wait_send()
            piece_copy(q, j).start()

            @pl.when(q == 1)
            def _():
                slot_copy(j).start()

        @pl.when(q < PIECES - 1)
        def _():
            arrange(q + 1)

        for step in range(4):

            @pl.when(q == step + 2)
            def _():
                moment_merge(step)

        return carry

    lax.fori_loop(1, PIECES, run, 0)
    for j in range(peers - 1):
        piece_copy(PIECES - 1, j).wait_send()
        slot_copy(j).wait_send()
    others = pl.ds(0, peers - 1)
    pltpu.make_async_copy(slots_ref.at[others], slots_ref.at[others], slot_recv).wait()
    pltpu.make_async_copy(land_ref.at[others], land_ref.at[others], land_sem).wait()


def finish_kernel(land_ref, slots_ref, stat_ref, out_hbm, mom_ref, ready, out_sem):
    peers, rows, width = land_ref.shape
    tiles = width // LANES
    row = lambda ref, first: jnp.concatenate([ref[pl.ds(first + t, 1)] for t in range(tiles)], axis=1)
    center, variance = row(stat_ref, 0), row(stat_ref, tiles)
    mom_ref[pl.ds(0, 1)] = center
    mom_ref[pl.ds(1, 1)] = variance
    factor = lax.rsqrt(variance + eps_value)
    center = jnp.broadcast_to(center, (8, width))
    factor = jnp.broadcast_to(factor, (8, width))

    def block(s, carry):
        for r in range(0, rows, 8):
            scaled = (land_ref[s, pl.ds(r, 8)] - center) * factor
            ready[s, pl.ds(r, 8)] = jnp.clip(scaled, -clip_value, clip_value)
        pltpu.make_async_copy(ready.at[s], out_hbm.at[slots_ref[s, 0]], out_sem).start()
        return carry

    lax.fori_loop(0, peers, block, 0)
    pltpu.make_async_copy(ready, out_hbm, out_sem).wait()


def body(features, dest, slot):
    row_count, width = features.shape
    peers = lax.axis_size("inner")
    blocks = dest.shape[0]
    rows = row_count // blocks
    tiles = width // LANES
    vmem = pl.BlockSpec(memory_space=pltpu.VMEM)
    hbm = pl.BlockSpec(memory_space=pltpu.HBM)
    smem = pl.BlockSpec(memory_space=pltpu.SMEM)
    operands = (
        dest.reshape(1, blocks),
        slot.reshape(1, blocks),
        features.reshape(blocks, rows, width),
    )
    landed, slots, stats = pl.pallas_call(
        exchange_kernel,
        out_shape=[
            pltpu.VMEM((peers, rows, width), jnp.float32),
            pltpu.VMEM((peers, LANES), jnp.int32),
            pltpu.VMEM((2 * tiles, LANES), jnp.float32),
        ],
        in_specs=[hbm, hbm, hbm],
        out_specs=[vmem, vmem, vmem],
        scratch_shapes=[
            pltpu.VMEM((blocks, rows, width), jnp.float32),
            pltpu.VMEM((peers, rows, width), jnp.float32),
            pltpu.VMEM((1, blocks), jnp.int32),
            pltpu.VMEM((1, blocks), jnp.int32),
            pltpu.VMEM((peers, LANES), jnp.int32),
            pltpu.VMEM((peers, LANES), jnp.int32),
            pltpu.SMEM((peers, LANES), jnp.int32),
            pltpu.VMEM((4, 2 * tiles, LANES), jnp.float32),
            pltpu.VMEM((10, 2 * tiles, LANES), jnp.float32),
            pltpu.SemaphoreType.DMA((LOADS + 3,)),
            pltpu.SemaphoreType.DMA((peers - 1,)),
            pltpu.SemaphoreType.DMA,
            pltpu.SemaphoreType.DMA((peers - 1,)),
            pltpu.SemaphoreType.DMA,
            pltpu.SemaphoreType.DMA((10,)),
            pltpu.SemaphoreType.DMA((10,)),
        ],
        compiler_params=pltpu.CompilerParams(
            collective_id=0, has_side_effects=True, vmem_limit_bytes=48 * 2**20
        ),
    )(*(pltpu.with_memory_space_constraint(a, pltpu.HBM) for a in operands))
    standardized, moments = pl.pallas_call(
        finish_kernel,
        out_shape=[
            jax.ShapeDtypeStruct((peers, rows, width), jnp.float32),
            jax.ShapeDtypeStruct((2, width), jnp.float32),
        ],
        in_specs=[vmem, smem, vmem],
        out_specs=[hbm, vmem],
        scratch_shapes=[
            pltpu.VMEM((peers, rows, width), jnp.float32),
            pltpu.SemaphoreType.DMA,
        ],
        compiler_params=pltpu.CompilerParams(vmem_limit_bytes=24 * 2**20),
    )(landed, slots, stats)
    return (standardized.reshape(row_count, width), moments)


def solution(mesh):
    in_specs = (P(("outer", "inner"), None), P(("outer", "inner")), P(("outer", "inner")))
    out_specs = (P(("outer", "inner"), None), P())
    return jax.shard_map(body, mesh=mesh, in_specs=in_specs, out_specs=out_specs, check_vma=False)
```

```python
import itertools

import jax
import jax.numpy as jnp
from jax import lax
from jax.experimental import pallas as pl
from jax.experimental.pallas import tpu as pltpu
from jax.sharding import PartitionSpec as P

MESH = pl.DeviceIdType.MESH
eps_value = 1e-06
clip_value = 3.0
SIDE = 4
PIECES = 8
LOADS = 4
LANES = 128


def hops(offset):
    return sum(min(v, SIDE - v) for v in offset)


def axes(offset):
    return sum(v != 0 for v in offset)


def send_order():
    left = [d for d in itertools.product(range(SIDE), repeat=3) if any(d)]
    groups = []
    while left:
        first, group = left[0], []
        for shift in range(3):
            for sign in (1, -1):
                d = tuple(sign * first[(j + shift) % 3] % SIDE for j in range(3))
                if d in left:
                    left.remove(d)
                    group.append(d)
        groups.append(group)
    return [d for group in sorted(groups, key=lambda g: (axes(g[0]), hops(g[0]))) for d in group]


def close_count():
    return sum(axes(d) == 1 for d in send_order())


def merge_pair(a, b, half):
    gap = b[0] - a[0]
    return ((a[0] + b[0]) * 0.5, a[1] + b[1] + gap * gap * half)


def exchange_kernel(
    dest_hbm, slot_hbm, feat_hbm,
    land_ref, slots_ref, stat_ref,
    feats_0, feats_1, feats_2, feats_3, stage, stage_close, dest_v, slot_v, order_v, slots_v, slots_in, order_s, moment, peer_moment,
    two_sem, three_sem, load_sem, send_sem, land_sem, slot_send, slot_recv, mom_send, mom_recv,
):
    peers, rows, width = land_ref.shape
    tiles = width // LANES
    col_pieces = PIECES * 8 // rows
    cols = width // col_pieces
    core, me = lax.axis_index("outer"), lax.axis_index("inner")
    y, x, z = me // (SIDE * SIDE), (me // SIDE) % SIDE, me % SIDE

    def at(offset):
        dy, dx, dz = offset
        return ((y + dy) % SIDE) * SIDE * SIDE + ((x + dx) % SIDE) * SIDE + (z + dz) % SIDE

    barrier = pltpu.get_barrier_semaphore()
    feats = (feats_0, feats_1, feats_2, feats_3)
    load = peers // LOADS
    loads = [
        [
            pltpu.make_async_copy(
                feat_hbm.at[pl.ds(k * load, load), pl.ds(r * 8, 8)],
                feats[r].at[pl.ds(k * load, load)],
                load_sem.at[r * LOADS + k],
            )
            for k in range(LOADS)
        ]
        for r in range(len(feats))
    ]
    small = [
        pltpu.make_async_copy(dest_hbm, dest_v, load_sem.at[4 * LOADS]),
        pltpu.make_async_copy(slot_hbm, slot_v, load_sem.at[4 * LOADS + 1]),
    ]
    for copy in small + loads[0]:
        copy.start()

    order_of = send_order()
    targets = [at(d) for d in order_of]
    close = close_count()
    planar = sum(axes(d) <= 2 for d in order_of)

    def greet(semaphore):
        for j in range(close):
            pl.semaphore_signal(semaphore, inc=1, device_id=(core, targets[j]), device_id_type=MESH)

    greet(barrier)
    pl.semaphore_signal(barrier, inc=1, device_id=(1 - core, me), device_id_type=MESH)
    for group in loads[1:]:
        for copy in group:
            copy.start()

    for copy in small:
        copy.wait()
    blocks = dest_v.shape[1]
    hit = dest_v[...] == lax.broadcasted_iota(jnp.int32, (peers, blocks), 0)
    ids = lax.broadcasted_iota(jnp.int32, (peers, blocks), 1)
    order = jnp.max(jnp.where(hit, ids, 0), axis=1, keepdims=True)
    slots = jnp.max(jnp.where(hit, slot_v[...], 0), axis=1, keepdims=True)
    order_v[...] = jnp.broadcast_to(order, order_v.shape)
    slots_v[...] = jnp.broadcast_to(slots, slots_v.shape)
    to_scalar = pltpu.make_async_copy(order_v, order_s, load_sem.at[4 * LOADS + 2])
    to_scalar.start()
    slots_in[pl.ds(me, 1)] = slots_v[pl.ds(me, 1)]

    def part(q):
        return pl.ds((q // col_pieces) * 8, 8), pl.ds(pl.multiple_of((q % col_pieces) * cols, cols), cols)

    def arrange(q, r):
        def one(p, carry):
            stage[(p,) + part(q)] = feats[r][order_s[p, 0], :, part(q)[1]]
            return carry

        lax.fori_loop(0, peers, one, 0, unroll=8)

    def slot_copy(j):
        return pltpu.make_async_remote_copy(
            src_ref=slots_v.at[pl.ds(targets[j], 1)],
            dst_ref=slots_in.at[pl.ds(me, 1)],
            send_sem=slot_send.at[j],
            recv_sem=slot_recv,
            device_id=(core, targets[j]),
            device_id_type=MESH,
        )

    def block_copy(j, where):
        return pltpu.make_async_remote_copy(
            src_ref=stage_close.at[(j,) + where] if j < close else stage.at[(targets[j],) + where],
            dst_ref=land_ref.at[(me,) + where],
            send_sem=send_sem.at[j],
            recv_sem=land_sem,
            device_id=(core, targets[j]),
            device_id_type=MESH,
        )

    def piece_copy(q, j):
        return block_copy(j, part(q))

    def read(ref):
        return ref[pl.ds(0, tiles)], ref[pl.ds(tiles, tiles)]

    def write(ref, pair):
        ref[pl.ds(0, tiles)] = pair[0]
        ref[pl.ds(tiles, tiles)] = pair[1]

    def moment_copies(step):
        if step == 3:
            mates = [(1 - core, me)]
        else:
            mates = [(core, me ^ (k * SIDE**step)) for k in (1, 2, 3)]
        return [
            pltpu.make_async_remote_copy(
                src_ref=moment.at[step],
                dst_ref=peer_moment.at[step * 3 + k],
                send_sem=mom_send.at[step * 3 + k],
                recv_sem=mom_recv.at[step * 3 + k],
                device_id=mate,
                device_id_type=MESH,
            )
            for k, mate in enumerate(mates)
        ]

    def moment_send(step):
        for copy in moment_copies(step):
            copy.start()

    def moment_merge(step):
        for copy in moment_copies(step):
            copy.wait()
        count = float(peers * rows * SIDE**step)
        pair = merge_pair(read(moment.at[step]), read(peer_moment.at[step * 3]), count * 0.5)
        if step < 3:
            other = merge_pair(
                read(peer_moment.at[step * 3 + 1]), read(peer_moment.at[step * 3 + 2]), count * 0.5
            )
            pair = merge_pair(pair, other, count)
            write(moment.at[step + 1], pair)
            moment_send(step + 1)
        else:
            write(stat_ref, (pair[0], pair[1] / (count * 2.0)))

    pl.semaphore_wait(barrier, close + 1)
    greet(two_sem)
    to_scalar.wait()
    for r in range(len(feats)):
        where = pl.ds(r * 8, 8)
        for copy in loads[r]:
            copy.wait()
        for j in range(close):
            stage_close[j, where] = feats[r][order_s[targets[j], 0]]
            block_copy(j, (where,)).start()
        if r == 0:
            arrange(0, 0)
    pl.semaphore_wait(two_sem, close)
    greet(three_sem)
    for j in range(close, planar):
        piece_copy(0, j).start()
    pl.semaphore_wait(three_sem, close)
    for j in range(planar, peers - 1):
        piece_copy(0, j).start()
    arrange(1, 1 // col_pieces)

    zero = jnp.zeros((8, width), jnp.float32)
    acc = zero
    for feat in feats:
        acc = lax.fori_loop(0, peers, lambda b, acc: acc + feat[b], acc, unroll=2)
    center = jnp.sum(acc, axis=0, keepdims=True) * (1.0 / (peers * rows))
    wide = jnp.broadcast_to(center, (8, width))
    acc = zero
    for feat in feats:

        def squares(b, acc):
            gap = feat[b] - wide
            return acc + gap * gap

        acc = lax.fori_loop(0, peers, squares, acc, unroll=2)
    spread = jnp.sum(acc, axis=0, keepdims=True)
    for t in range(tiles):
        moment[0, pl.ds(t, 1)] = center[:, t * LANES : (t + 1) * LANES]
        moment[0, pl.ds(tiles + t, 1)] = spread[:, t * LANES : (t + 1) * LANES]
    moment_send(0)
    for r in range(len(feats)):
        land_ref[me, pl.ds(r * 8, 8)] = feats[r][order_s[me, 0]]

    def run(q, carry):
        for j in range(close, peers - 1):
            piece_copy(q - 1, j).wait_send()
            piece_copy(q, j).start()

        @pl.when(q == 1)
        def _():
            for j in range(peers - 1):
                slot_copy(j).start()

        for r in range(len(feats)):

            @pl.when((q + 1) // col_pieces == r)
            def _():
                arrange(q + 1, r)

        for step in range(4):

            @pl.when(q == step + 2)
            def _():
                moment_merge(step)

        return carry

    lax.fori_loop(1, PIECES, run, 0)
    others = pl.ds(0, peers - 1)
    pltpu.make_async_copy(slots_in.at[others], slots_in.at[others], slot_recv).wait()
    pltpu.sync_copy(slots_in, slots_ref)
    for j in range(close):
        block_copy(j, ()).wait_send()
    for j in range(close, peers - 1):
        piece_copy(PIECES - 1, j).wait_send()
    for j in range(peers - 1):
        slot_copy(j).wait_send()
    pltpu.make_async_copy(land_ref.at[others], land_ref.at[others], land_sem).wait()


def finish_kernel(land_ref, slots_ref, stat_ref, out_hbm, mom_hbm, ready, mom, out_sem, mom_sem):
    peers, rows, width = land_ref.shape
    tiles = width // LANES
    row = lambda ref, first: jnp.concatenate([ref[pl.ds(first + t, 1)] for t in range(tiles)], axis=1)
    center, variance = row(stat_ref, 0), row(stat_ref, tiles)
    mom[pl.ds(0, 1)] = center
    mom[pl.ds(1, 1)] = variance
    mom_copy = pltpu.make_async_copy(mom, mom_hbm, mom_sem)
    mom_copy.start()
    factor = lax.rsqrt(variance + eps_value)
    center = jnp.broadcast_to(center, (8, width))
    factor = jnp.broadcast_to(factor, (8, width))

    def block(s, carry):
        for r in range(0, rows, 8):
            scaled = (land_ref[s, pl.ds(r, 8)] - center) * factor
            ready[s, pl.ds(r, 8)] = jnp.clip(scaled, -clip_value, clip_value)
        pltpu.make_async_copy(ready.at[s], out_hbm.at[slots_ref[s, 0]], out_sem).start()
        return carry

    lax.fori_loop(0, peers, block, 0)
    mom_copy.wait()
    pltpu.make_async_copy(ready, out_hbm, out_sem).wait()


def body(features, dest, slot):
    row_count, width = features.shape
    peers = lax.axis_size("inner")
    blocks = dest.shape[0]
    rows = row_count // blocks
    tiles = width // LANES
    vmem = pl.BlockSpec(memory_space=pltpu.VMEM)
    hbm = pl.BlockSpec(memory_space=pltpu.HBM)
    smem = pl.BlockSpec(memory_space=pltpu.SMEM)
    operands = (
        dest.reshape(1, blocks),
        slot.reshape(1, blocks),
        features.reshape(blocks, rows, width),
    )
    landed, slots, stats = pl.pallas_call(
        exchange_kernel,
        out_shape=[
            pltpu.VMEM((peers, rows, width), jnp.float32),
            pltpu.SMEM((peers, LANES), jnp.int32),
            pltpu.VMEM((2 * tiles, LANES), jnp.float32),
        ],
        in_specs=[hbm, hbm, hbm],
        out_specs=[vmem, smem, vmem],
        scratch_shapes=[
            pltpu.VMEM((blocks, 8, width), jnp.float32),
            pltpu.VMEM((blocks, 8, width), jnp.float32),
            pltpu.VMEM((blocks, 8, width), jnp.float32),
            pltpu.VMEM((blocks, 8, width), jnp.float32),
            pltpu.VMEM((peers, rows, width), jnp.float32),
            pltpu.VMEM((close_count(), rows, width), jnp.float32),
            pltpu.VMEM((1, blocks), jnp.int32),
            pltpu.VMEM((1, blocks), jnp.int32),
            pltpu.VMEM((peers, LANES), jnp.int32),
            pltpu.VMEM((peers, LANES), jnp.int32),
            pltpu.VMEM((peers, LANES), jnp.int32),
            pltpu.SMEM((peers, LANES), jnp.int32),
            pltpu.VMEM((4, 2 * tiles, LANES), jnp.float32),
            pltpu.VMEM((10, 2 * tiles, LANES), jnp.float32),
            pltpu.SemaphoreType.REGULAR,
            pltpu.SemaphoreType.REGULAR,
            pltpu.SemaphoreType.DMA((4 * LOADS + 3,)),
            pltpu.SemaphoreType.DMA((peers - 1,)),
            pltpu.SemaphoreType.DMA,
            pltpu.SemaphoreType.DMA((peers - 1,)),
            pltpu.SemaphoreType.DMA,
            pltpu.SemaphoreType.DMA((10,)),
            pltpu.SemaphoreType.DMA((10,)),
        ],
        compiler_params=pltpu.CompilerParams(
            collective_id=0, has_side_effects=True, vmem_limit_bytes=48 * 2**20
        ),
    )(*(pltpu.with_memory_space_constraint(a, pltpu.HBM) for a in operands))
    standardized, moments = pl.pallas_call(
        finish_kernel,
        out_shape=[
            jax.ShapeDtypeStruct((peers, rows, width), jnp.float32),
            jax.ShapeDtypeStruct((2, width), jnp.float32),
        ],
        in_specs=[vmem, smem, vmem],
        out_specs=[hbm, hbm],
        scratch_shapes=[
            pltpu.VMEM((peers, rows, width), jnp.float32),
            pltpu.VMEM((2, width), jnp.float32),
            pltpu.SemaphoreType.DMA,
            pltpu.SemaphoreType.DMA,
        ],
        compiler_params=pltpu.CompilerParams(vmem_limit_bytes=24 * 2**20),
    )(landed, slots, stats)
    return (standardized.reshape(row_count, width), moments)


def solution(mesh):
    in_specs = (P(("outer", "inner"), None), P(("outer", "inner")), P(("outer", "inner")))
    out_specs = (P(("outer", "inner"), None), P())
    return jax.shard_map(body, mesh=mesh, in_specs=in_specs, out_specs=out_specs, check_vma=False)
```

```python
import itertools

import jax
import jax.numpy as jnp
from jax import lax
from jax.experimental import pallas as pl
from jax.experimental.pallas import tpu as pltpu
from jax.sharding import PartitionSpec as P

MESH = pl.DeviceIdType.MESH
eps_value = 1e-06
clip_value = 3.0
SIDE = 4
PIECES = 8
LOADS = 2
LANES = 128


def hops(offset):
    return sum(min(v, SIDE - v) for v in offset)


def axes(offset):
    return sum(v != 0 for v in offset)


def send_order():
    left = [d for d in itertools.product(range(SIDE), repeat=3) if any(d)]
    groups = []
    while left:
        first, group = left[0], []
        for shift in range(3):
            for sign in (1, -1):
                d = tuple(sign * first[(j + shift) % 3] % SIDE for j in range(3))
                if d in left:
                    left.remove(d)
                    group.append(d)
        groups.append(group)
    return [d for group in sorted(groups, key=lambda g: (axes(g[0]), hops(g[0]))) for d in group]


def close_count():
    return sum(axes(d) == 1 for d in send_order())


def merge_pair(a, b, half):
    gap = b[0] - a[0]
    return ((a[0] + b[0]) * 0.5, a[1] + b[1] + gap * gap * half)


def exchange_kernel(
    dest_hbm, slot_hbm, feat_hbm,
    land_ref, slots_ref, stat_ref,
    feats_0, feats_1, feats_2, feats_3, stage, stage_close, dest_v, slot_v, order_v, slots_v, slots_in, order_s, moment, peer_moment,
    two_sem, three_sem, load_sem, send_sem, land_sem, slot_send, slot_recv, mom_send, mom_recv,
):
    peers, rows, width = land_ref.shape
    tiles = width // LANES
    col_pieces = PIECES * 8 // rows
    cols = width // col_pieces
    core, me = lax.axis_index("outer"), lax.axis_index("inner")
    y, x, z = me // (SIDE * SIDE), (me // SIDE) % SIDE, me % SIDE

    def at(offset):
        dy, dx, dz = (a + core * (b - a) for a, b in zip(offset, offset[1:] + offset[:1]))
        return ((y + dy) % SIDE) * SIDE * SIDE + ((x + dx) % SIDE) * SIDE + (z + dz) % SIDE

    barrier = pltpu.get_barrier_semaphore()
    feats = (feats_0, feats_1, feats_2, feats_3)
    load = peers // LOADS
    loads = [
        [
            pltpu.make_async_copy(
                feat_hbm.at[pl.ds(k * load, load), pl.ds(r * 8, 8)],
                feats[r].at[pl.ds(k * load, load)],
                load_sem.at[r * LOADS + k],
            )
            for k in range(LOADS)
        ]
        for r in range(len(feats))
    ]
    small = [
        pltpu.make_async_copy(dest_hbm, dest_v, load_sem.at[4 * LOADS]),
        pltpu.make_async_copy(slot_hbm, slot_v, load_sem.at[4 * LOADS + 1]),
    ]
    order_of = send_order()
    targets = [at(d) for d in order_of]
    close = close_count()
    planar = sum(axes(d) <= 2 for d in order_of)

    def greet(semaphore):
        for j in range(close):
            pl.semaphore_signal(semaphore, inc=1, device_id=(core, targets[j]), device_id_type=MESH)

    greet(barrier)
    pl.semaphore_signal(barrier, inc=1, device_id=(1 - core, me), device_id_type=MESH)
    for copy in small + loads[0]:
        copy.start()
    for group in loads[1:]:
        for copy in group:
            copy.start()

    for copy in small:
        copy.wait()
    blocks = dest_v.shape[1]
    hit = dest_v[...] == lax.broadcasted_iota(jnp.int32, (peers, blocks), 0)
    ids = lax.broadcasted_iota(jnp.int32, (peers, blocks), 1)
    order = jnp.max(jnp.where(hit, ids, 0), axis=1, keepdims=True)
    slots = jnp.max(jnp.where(hit, slot_v[...], 0), axis=1, keepdims=True)
    same = lax.broadcasted_iota(jnp.int32, (peers, peers), 0) == lax.broadcasted_iota(jnp.int32, (peers, peers), 1)
    order_v[...] = jnp.max(jnp.where(same, order, 0), axis=0, keepdims=True)
    slots_v[...] = jnp.broadcast_to(slots, slots_v.shape)
    to_scalar = pltpu.make_async_copy(order_v, order_s, load_sem.at[4 * LOADS + 2])
    to_scalar.start()
    dest_row, ids_row = dest_v[...], lax.broadcasted_iota(jnp.int32, (1, blocks), 1)
    sources = [jnp.max(jnp.where(dest_row == targets[j], ids_row, 0)) for j in range(close)]
    slots_in[pl.ds(me, 1)] = slots_v[pl.ds(me, 1)]

    def part(q):
        return pl.ds((q // col_pieces) * 8, 8), pl.ds(pl.multiple_of((q % col_pieces) * cols, cols), cols)

    def arrange(q, r):
        def one(p, carry):
            stage[(p,) + part(q)] = feats[r][order_s[0, p], :, part(q)[1]]
            return carry

        lax.fori_loop(0, peers, one, 0, unroll=8)

    def slot_copy(j):
        return pltpu.make_async_remote_copy(
            src_ref=slots_v.at[pl.ds(targets[j], 1)],
            dst_ref=slots_in.at[pl.ds(me, 1)],
            send_sem=slot_send.at[j],
            recv_sem=slot_recv,
            device_id=(core, targets[j]),
            device_id_type=MESH,
        )

    def block_copy(j, where):
        return pltpu.make_async_remote_copy(
            src_ref=stage_close.at[(j,) + where] if j < close else stage.at[(targets[j],) + where],
            dst_ref=land_ref.at[(me,) + where],
            send_sem=send_sem.at[j],
            recv_sem=land_sem,
            device_id=(core, targets[j]),
            device_id_type=MESH,
        )

    def piece_copy(q, j):
        return block_copy(j, part(q))

    def read(ref):
        return ref[pl.ds(0, tiles)], ref[pl.ds(tiles, tiles)]

    def write(ref, pair):
        ref[pl.ds(0, tiles)] = pair[0]
        ref[pl.ds(tiles, tiles)] = pair[1]

    def moment_copies(step):
        if step == 3:
            mates = [(1 - core, me)]
        else:
            mates = [(core, me ^ (k * SIDE**step)) for k in (1, 2, 3)]
        return [
            pltpu.make_async_remote_copy(
                src_ref=moment.at[step],
                dst_ref=peer_moment.at[step * 3 + k],
                send_sem=mom_send.at[step * 3 + k],
                recv_sem=mom_recv.at[step * 3 + k],
                device_id=mate,
                device_id_type=MESH,
            )
            for k, mate in enumerate(mates)
        ]

    def moment_send(step):
        for copy in moment_copies(step):
            copy.start()

    def moment_merge(step):
        for copy in moment_copies(step):
            copy.wait()
        count = float(peers * rows * SIDE**step)
        pair = merge_pair(read(moment.at[step]), read(peer_moment.at[step * 3]), count * 0.5)
        if step < 3:
            other = merge_pair(
                read(peer_moment.at[step * 3 + 1]), read(peer_moment.at[step * 3 + 2]), count * 0.5
            )
            pair = merge_pair(pair, other, count)
            write(moment.at[step + 1], pair)
            moment_send(step + 1)
        else:
            write(stat_ref, (pair[0], pair[1] / (count * 2.0)))

    for r in range(len(feats)):
        where = pl.ds(r * 8, 8)
        for copy in loads[r]:
            copy.wait()
        for j in range(close):
            stage_close[j, where] = feats[r][sources[j]]
        if r == 0:
            pl.semaphore_wait(barrier, close + 1)
        for j in range(close):
            block_copy(j, (where,)).start()
        if r == 0:
            greet(two_sem)
            to_scalar.wait()
            arrange(0, 0)
    pl.semaphore_wait(two_sem, close)
    greet(three_sem)
    for j in range(close, planar):
        piece_copy(0, j).start()
    pl.semaphore_wait(three_sem, close)
    for j in range(planar, peers - 1):
        piece_copy(0, j).start()
    arrange(1, 1 // col_pieces)

    zero = jnp.zeros((8, width), jnp.float32)
    acc = zero
    for feat in feats:
        acc = lax.fori_loop(0, peers, lambda b, acc: acc + feat[b], acc, unroll=2)
    center = jnp.sum(acc, axis=0, keepdims=True) * (1.0 / (peers * rows))
    wide = jnp.broadcast_to(center, (8, width))
    acc = zero
    for feat in feats:

        def squares(b, acc):
            gap = feat[b] - wide
            return acc + gap * gap

        acc = lax.fori_loop(0, peers, squares, acc, unroll=2)
    spread = jnp.sum(acc, axis=0, keepdims=True)
    for t in range(tiles):
        moment[0, pl.ds(t, 1)] = center[:, t * LANES : (t + 1) * LANES]
        moment[0, pl.ds(tiles + t, 1)] = spread[:, t * LANES : (t + 1) * LANES]
    moment_send(0)
    for r in range(len(feats)):
        land_ref[me, pl.ds(r * 8, 8)] = feats[r][order_s[0, me]]

    def run(q, carry):
        for j in sorted(range(close, peers - 1), key=lambda j: hops(order_of[j])):
            piece_copy(q - 1, j).wait_send()
            piece_copy(q, j).start()

        @pl.when(q == 1)
        def _():
            for j in range(peers - 1):
                slot_copy(j).start()

        for r in range(len(feats)):

            @pl.when((q + 1) // col_pieces == r)
            def _():
                arrange(q + 1, r)

        for step in range(4):

            @pl.when(q == step + 2)
            def _():
                moment_merge(step)

        return carry

    lax.fori_loop(1, PIECES, run, 0)
    others = pl.ds(0, peers - 1)
    pltpu.make_async_copy(slots_in.at[others], slots_in.at[others], slot_recv).wait()
    pltpu.sync_copy(slots_in, slots_ref)
    for j in range(close):
        block_copy(j, ()).wait_send()
    for j in range(close, peers - 1):
        piece_copy(PIECES - 1, j).wait_send()
    for j in range(peers - 1):
        slot_copy(j).wait_send()
    pltpu.make_async_copy(land_ref.at[others], land_ref.at[others], land_sem).wait()


def finish_kernel(land_ref, slots_ref, stat_ref, out_hbm, mom_hbm, ready, mom, out_sem, mom_sem):
    peers, rows, width = land_ref.shape
    tiles = width // LANES
    row = lambda ref, first: jnp.concatenate([ref[pl.ds(first + t, 1)] for t in range(tiles)], axis=1)
    center, variance = row(stat_ref, 0), row(stat_ref, tiles)
    mom[pl.ds(0, 1)] = center
    mom[pl.ds(1, 1)] = variance
    mom_copy = pltpu.make_async_copy(mom, mom_hbm, mom_sem)
    mom_copy.start()
    factor = lax.rsqrt(variance + eps_value)
    center = jnp.broadcast_to(center, (8, width))
    factor = jnp.broadcast_to(factor, (8, width))

    def block(s, carry):
        for r in range(0, rows, 8):
            scaled = (land_ref[s, pl.ds(r, 8)] - center) * factor
            ready[s, pl.ds(r, 8)] = jnp.clip(scaled, -clip_value, clip_value)
        pltpu.make_async_copy(ready.at[s], out_hbm.at[slots_ref[s, 0]], out_sem).start()
        return carry

    lax.fori_loop(0, peers, block, 0)
    mom_copy.wait()
    pltpu.make_async_copy(ready, out_hbm, out_sem).wait()


def body(features, dest, slot):
    row_count, width = features.shape
    peers = lax.axis_size("inner")
    blocks = dest.shape[0]
    rows = row_count // blocks
    tiles = width // LANES
    vmem = pl.BlockSpec(memory_space=pltpu.VMEM)
    hbm = pl.BlockSpec(memory_space=pltpu.HBM)
    smem = pl.BlockSpec(memory_space=pltpu.SMEM)
    operands = (
        dest.reshape(1, blocks),
        slot.reshape(1, blocks),
        features.reshape(blocks, rows, width),
    )
    landed, slots, stats = pl.pallas_call(
        exchange_kernel,
        out_shape=[
            pltpu.VMEM((peers, rows, width), jnp.float32),
            pltpu.SMEM((peers, LANES), jnp.int32),
            pltpu.VMEM((2 * tiles, LANES), jnp.float32),
        ],
        in_specs=[hbm, hbm, hbm],
        out_specs=[vmem, smem, vmem],
        scratch_shapes=[
            pltpu.VMEM((blocks, 8, width), jnp.float32),
            pltpu.VMEM((blocks, 8, width), jnp.float32),
            pltpu.VMEM((blocks, 8, width), jnp.float32),
            pltpu.VMEM((blocks, 8, width), jnp.float32),
            pltpu.VMEM((peers, rows, width), jnp.float32),
            pltpu.VMEM((close_count(), rows, width), jnp.float32),
            pltpu.VMEM((1, blocks), jnp.int32),
            pltpu.VMEM((1, blocks), jnp.int32),
            pltpu.VMEM((1, peers), jnp.int32),
            pltpu.VMEM((peers, LANES), jnp.int32),
            pltpu.VMEM((peers, LANES), jnp.int32),
            pltpu.SMEM((1, peers), jnp.int32),
            pltpu.VMEM((4, 2 * tiles, LANES), jnp.float32),
            pltpu.VMEM((10, 2 * tiles, LANES), jnp.float32),
            pltpu.SemaphoreType.REGULAR,
            pltpu.SemaphoreType.REGULAR,
            pltpu.SemaphoreType.DMA((4 * LOADS + 3,)),
            pltpu.SemaphoreType.DMA((peers - 1,)),
            pltpu.SemaphoreType.DMA,
            pltpu.SemaphoreType.DMA((peers - 1,)),
            pltpu.SemaphoreType.DMA,
            pltpu.SemaphoreType.DMA((10,)),
            pltpu.SemaphoreType.DMA((10,)),
        ],
        compiler_params=pltpu.CompilerParams(
            collective_id=0, has_side_effects=True, vmem_limit_bytes=48 * 2**20
        ),
    )(*(pltpu.with_memory_space_constraint(a, pltpu.HBM) for a in operands))
    standardized, moments = pl.pallas_call(
        finish_kernel,
        out_shape=[
            jax.ShapeDtypeStruct((peers, rows, width), jnp.float32),
            jax.ShapeDtypeStruct((2, width), jnp.float32),
        ],
        in_specs=[vmem, smem, vmem],
        out_specs=[hbm, hbm],
        scratch_shapes=[
            pltpu.VMEM((peers, rows, width), jnp.float32),
            pltpu.VMEM((2, width), jnp.float32),
            pltpu.SemaphoreType.DMA,
            pltpu.SemaphoreType.DMA,
        ],
        compiler_params=pltpu.CompilerParams(vmem_limit_bytes=24 * 2**20),
    )(landed, slots, stats)
    return (standardized.reshape(row_count, width), moments)


def solution(mesh):
    in_specs = (P(("outer", "inner"), None), P(("outer", "inner")), P(("outer", "inner")))
    out_specs = (P(("outer", "inner"), None), P())
    return jax.shard_map(body, mesh=mesh, in_specs=in_specs, out_specs=out_specs, check_vma=False)
```
